1024 devices in a mesh: outer: 8 (over x, core), inner: 128 (over y, z).
Axes of the slice: x: 4, y: 4, z: 32, core: 2. Of those that a mesh axis runs over, the one named last changes fastest.
Arguments:
- queries: bfloat16 [131072, 4096], P(('outer', 'inner')), may hold values from -200 to 200
- keys: bfloat16 [131072, 1024], P(('outer', 'inner')), may hold values from -6 to 6
- values: bfloat16 [131072, 1024], P(('outer', 'inner')), may hold values from -6 to 6
- lengths: int32 [256], replicated, may hold values from 1 to 1024, as said below
- pack_order: int32 [256], replicated, may hold values from 0 to 255, as said below
Outputs:
- attended: bfloat16 [131072, 4096], P(('outer', 'inner'))
The draws below stay inside these ranges and needn't reach their ends.
Inputs may be any that keep to these rules, and one draw needn't show every extreme that they name: 256 lengths that sum to 131072; the document packed first, lengths[pack_order[0]], has exactly 1024 tokens. `pack_order`: each of 0 to 255 exactly once.
All inputs are finite; a program needn't handle non-finite values.
Results may differ from the reference program's by a relative error of at most 0.0046.
Values may be sent and summed in bfloat16 or wider, within the bound.
A program may use at most 64 MiB of HBM per device.

```python
import jax
import jax.numpy as jnp
from jax import lax

HEADS = 32
KV_HEADS = 8
HD = 128
TOK_DEV = 128
HOPS = 8
MOST = 1024
TOKENS = 131072
NDOC = 256


def drawn_pair(key):
    keys_base = jnp.clip(jax.random.normal(jax.random.fold_in(key, 11), (TOKENS, KV_HEADS * HD), jnp.float32), -6.0, 6.0)
    queries_base = jnp.clip(jax.random.normal(jax.random.fold_in(key, 12), (TOKENS, HEADS * HD), jnp.float32), -6.0, 6.0)
    return (queries_base, keys_base)


def draw_queries(key, part):
    return drawn_pair(key)[0].astype(jnp.bfloat16)


def draw_keys(key, part):
    return drawn_pair(key)[1].astype(jnp.bfloat16)


def packed_documents(key):
    others = NDOC - 1
    remaining = TOKENS - MOST
    quotient = remaining // others
    leftover = remaining % others
    spread = max(min(quotient - 1, MOST - quotient - 1), 0)
    pairs = others // 2
    base = quotient + (jnp.arange(others, dtype=jnp.int32) < leftover).astype(jnp.int32)
    delta = jax.random.randint(jax.random.fold_in(key, 21), (pairs,), 0, spread + 1, dtype=jnp.int32)
    signed = jnp.concatenate([delta, -delta, jnp.zeros((others - 2 * pairs,), jnp.int32)])
    rest = jax.random.permutation(jax.random.fold_in(key, 22), (base + signed).astype(jnp.int32))
    in_order = jnp.concatenate([jnp.full((1,), MOST, jnp.int32), rest.astype(jnp.int32)])
    order = jax.random.permutation(jax.random.fold_in(key, 23), NDOC).astype(jnp.int32)
    lengths = jnp.zeros((NDOC,), jnp.int32).at[order].set(in_order)
    return (lengths, order)


def draw_lengths(key, part):
    return packed_documents(key)[0]


def draw_pack_order(key, part):
    return packed_documents(key)[1]


def levels(key, dims, cuts, smallest, high):
    gain, own = 1.0, jax.random.fold_in(key, 6)
    for position, parts in cuts:
        draws = jnp.exp(jax.random.uniform(jax.random.fold_in(own, position), (parts,), jnp.float32, smallest / len(cuts), high / len(cuts)))
        gain = gain * jnp.repeat(draws, dims[position] // parts).reshape([-1 if axis == position else 1 for axis in range(len(dims))])
    return gain


def gaussian(own_key, shape, scale, bound, pieces=(), kind=jnp.bfloat16):
    array = scale * jax.random.normal(own_key, shape, jnp.float32)
    if pieces:
        array = array * levels(own_key, shape, pieces, -0.22, 0.18)
    return jnp.clip(array, -bound, bound).astype(kind)


def setup_inputs(seed: int = 0) -> dict:
    streams_of = jax.random.split(jax.random.key(seed), 6)
    return {
        "queries": draw_queries(jax.random.fold_in(streams_of[5], 71), 0),
        "keys": draw_keys(jax.random.fold_in(streams_of[5], 71), 0),
        "values": gaussian(streams_of[2], (TOKENS, KV_HEADS * HD), 1.0, 6.0, ((0, 1024),)),
        "lengths": draw_lengths(jax.random.fold_in(streams_of[5], 71), 0),
        "pack_order": draw_pack_order(jax.random.fold_in(streams_of[5], 71), 0),
    }


def segment_ids(lengths, pack_order, positions):
    placed = jnp.take(lengths, pack_order).astype(jnp.int32)
    doc_starts = (jnp.cumsum(placed) - placed).astype(jnp.int32)
    counted = (doc_starts[None, :] <= positions[:, None]).astype(jnp.int32)
    return lax.optimization_barrier(jnp.sum(counted, axis=1)).astype(jnp.int32) - 1

def reference(queries, keys, values, lengths, pack_order):
    shard_rows = TOK_DEV
    window = (HOPS + 1) * shard_rows
    group_size = HEADS // KV_HEADS
    padding = HOPS * shard_rows
    blocks_all = TOKENS // shard_rows
    key_pad = jnp.concatenate([jnp.zeros((padding, KV_HEADS * HD), keys.dtype), keys], axis=0)
    value_pad = jnp.concatenate([jnp.zeros((padding, KV_HEADS * HD), values.dtype), values], axis=0)

    def one_block(block_index):
        first_row = (block_index * shard_rows).astype(jnp.int32)
        query_rows = lax.dynamic_slice_in_dim(queries, first_row, shard_rows, 0)
        query_rows = query_rows.astype(jnp.float32).reshape(shard_rows, KV_HEADS, group_size, HD)
        key_rows = lax.dynamic_slice_in_dim(key_pad, first_row, window, 0)
        key_rows = key_rows.astype(jnp.float32).reshape(window, KV_HEADS, HD)
        value_rows = lax.dynamic_slice_in_dim(value_pad, first_row, window, 0)
        value_rows = value_rows.astype(jnp.float32).reshape(window, KV_HEADS, HD)
        query_pos = first_row + jnp.arange(shard_rows, dtype=jnp.int32)
        key_pos = first_row - padding + jnp.arange(window, dtype=jnp.int32)
        query_seg = segment_ids(lengths, pack_order, query_pos)
        key_seg = segment_ids(lengths, pack_order, key_pos)
        allowed = (key_pos[None, :] >= 0) & (key_pos[None, :] <= query_pos[:, None]) & (key_seg[None, :] == query_seg[:, None])
        scores = jnp.einsum('tgjd,kgd->gjtk', query_rows, key_rows) / jnp.sqrt(jnp.float32(HD))
        scores = jnp.where(allowed[None, None], scores, -jnp.inf)
        largest = lax.optimization_barrier(jnp.max(scores, axis=-1, keepdims=True))
        exps = jnp.exp(scores - largest)
        weights = (exps / lax.optimization_barrier(jnp.sum(exps, axis=-1, keepdims=True))).astype(jnp.bfloat16)
        weights = lax.optimization_barrier(weights).astype(jnp.float32)
        output = jnp.einsum('gjtk,kgd->tgjd', weights, value_rows)
        return output.reshape(shard_rows, HEADS * HD).astype(jnp.bfloat16)
    result = lax.map(one_block, jnp.arange(blocks_all, dtype=jnp.int32))
    return result.reshape(TOKENS, HEADS * HD)
```

```python
import functools
import math

import jax
import jax.numpy as jnp
from jax import lax
from jax.experimental import pallas as pl
from jax.experimental.pallas import tpu as pltpu
from jax.sharding import PartitionSpec as P

HD = 128
HOPS = 8
MESH = pl.DeviceIdType.MESH
SCALE = math.log2(math.e) / math.sqrt(HD)


def kernel(sizes, q_hbm, k_hbm, v_hbm, len_hbm, ord_hbm, o_hbm,
           len_ref, ord_ref, q_buf, o_buf, kv, acc, m_buf, l_buf, rel_buf, doc_sem, q_sem, in_sem, out_sem, send_sem, recv_sem):
    n_outer, n_inner = sizes
    rows = q_hbm.shape[0]
    kv_heads = k_hbm.shape[1] // HD
    group = q_hbm.shape[1] // k_hbm.shape[1]
    ndoc = len_hbm.shape[1]
    outer, inner = lax.axis_index("outer"), lax.axis_index("inner")
    device = outer * n_inner + inner
    total = n_outer * n_inner
    after = lax.rem(device + 1, total)
    before = lax.rem(device + total - 1, total)
    right = (after // n_inner, lax.rem(after, n_inner))
    left = (before // n_inner, lax.rem(before, n_inner))

    def load(h, part):
        source = k_hbm if part == 0 else v_hbm
        columns = pl.ds(pl.multiple_of(h * HD, HD), HD)
        return pltpu.make_async_copy(source.at[:, columns], kv.at[0, h, part], in_sem.at[h, part])

    def give(h):
        columns = pl.ds(pl.multiple_of(h * group * HD, group * HD), group * HD)
        return pltpu.make_async_copy(o_buf.at[:, columns], o_hbm.at[:, columns], out_sem.at[h])

    def hop(d, h):
        return pltpu.make_async_remote_copy(
            src_ref=kv.at[d, h], dst_ref=kv.at[d + 1, h],
            send_sem=send_sem.at[d, h], recv_sem=recv_sem.at[d, h],
            device_id=right, device_id_type=MESH)

    @pl.loop(0, kv_heads)
    def _(h):
        load(h, 0).start()
        load(h, 1).start()

    len_copy = pltpu.make_async_copy(len_hbm, len_ref, doc_sem.at[0])
    ord_copy = pltpu.make_async_copy(ord_hbm, ord_ref, doc_sem.at[1])
    len_copy.start()
    ord_copy.start()
    q_copy = pltpu.make_async_copy(q_hbm, q_buf, q_sem)
    q_copy.start()

    barrier = pltpu.get_barrier_semaphore()
    for neighbour in (left, right):
        pl.semaphore_signal(barrier, inc=1, device_id=neighbour, device_id_type=MESH)
    pl.semaphore_wait(barrier, 2)

    @pl.loop(0, kv_heads)
    def _(h):
        load(h, 0).wait()
        load(h, 1).wait()
        hop(0, h).start()

    len_copy.wait()
    ord_copy.wait()
    sub = lax.broadcasted_iota(jnp.int32, (ndoc, ndoc), 0)
    lane = lax.broadcasted_iota(jnp.int32, (ndoc, ndoc), 1)
    lengths = jnp.broadcast_to(len_ref[...], (ndoc, ndoc))
    order = jnp.broadcast_to(ord_ref[...], (ndoc, ndoc))
    zero = jnp.zeros((ndoc, ndoc), jnp.float32)
    by_row = jnp.sum(jnp.where(sub == lane, lengths.astype(jnp.float32), zero), axis=1, keepdims=True)
    placed = jnp.sum(jnp.where(sub == order, jnp.broadcast_to(by_row, (ndoc, ndoc)), zero), axis=0, keepdims=True)
    placed = jnp.broadcast_to(placed, (ndoc, ndoc))
    placed = jnp.sum(jnp.where(sub == lane, placed, zero), axis=1, keepdims=True)
    placed = jnp.broadcast_to(placed, (ndoc, ndoc))
    starts = jnp.sum(jnp.where(sub < lane, placed, zero), axis=0, keepdims=True)
    first_row = (device * rows).astype(jnp.float32)
    starts = jnp.broadcast_to(starts - first_row, (rows, ndoc))
    token = lax.broadcasted_iota(jnp.int32, (rows, ndoc), 0).astype(jnp.float32)
    begin = jnp.max(jnp.where(starts <= token, starts, -first_row), axis=1, keepdims=True)
    rel_buf[...] = jnp.broadcast_to(begin, (rows, HD))

    q_copy.wait()
    key = lax.broadcasted_iota(jnp.int32, (rows, HD), 1).astype(jnp.float32)
    query = lax.broadcasted_iota(jnp.int32, (rows, HD), 0).astype(jnp.float32)

    def scores(d, h, mask):
        q = jnp.concatenate(
            [q_buf[:, pl.ds(pl.multiple_of((h * group + j) * HD, HD), HD)] for j in range(group)], axis=0)
        s = lax.dot_general(q, kv[d, h, 0], (((1,), (1,)), ((), ())), preferred_element_type=jnp.float32)
        s = jnp.where(mask[None], s.reshape(group, rows, HD), -jnp.inf)
        return s.reshape(group * rows, HD)

    def first(h, mask):
        s = scores(0, h, mask)
        m = jnp.max(s, axis=1, keepdims=True)
        p = jnp.exp2((s - m) * SCALE)
        m_buf[h] = m
        l_buf[h] = jnp.sum(p, axis=1, keepdims=True)
        acc[h] = jnp.dot(p.astype(jnp.bfloat16), kv[0, h, 1], preferred_element_type=jnp.float32)

    def later(d, h, mask):
        s = scores(d, h, mask)
        m_old = m_buf[h]
        m = jnp.maximum(m_old, jnp.max(s, axis=1, keepdims=True))
        p = jnp.exp2((s - m) * SCALE)
        alpha = jnp.exp2((m_old - m) * SCALE)
        total_p = alpha * l_buf[h] + jnp.sum(p, axis=1, keepdims=True)
        mixed = alpha * acc[h] + jnp.dot(p.astype(jnp.bfloat16), kv[d, h, 1], preferred_element_type=jnp.float32)
        return m, total_p, mixed

    own = (key >= rel_buf[...]) & (key <= query)

    @pl.loop(0, kv_heads)
    def _(h):
        first(h, own)

    @pl.loop(1, HOPS)
    def _(d):
        mask = key - (d * rows).astype(jnp.float32) >= rel_buf[...]

        @pl.loop(0, kv_heads)
        def _(h):
            hop(d - 1, h).wait_recv()
            hop(d, h).start()
            m, total_p, mixed = later(d, h, mask)
            m_buf[h] = m
            l_buf[h] = total_p
            acc[h] = mixed

    last = key - float(HOPS * rows) >= rel_buf[...]

    @pl.loop(0, kv_heads)
    def _(h):
        hop(HOPS - 1, h).wait_recv()
        m, total_p, mixed = later(HOPS, h, last)
        out = (mixed / total_p).astype(o_buf.dtype)
        for j in range(group):
            o_buf[:, pl.ds(pl.multiple_of((h * group + j) * HD, HD), HD)] = out[j * rows:(j + 1) * rows]
        give(h).start()

    @pl.loop(0, HOPS)
    def _(d):
        @pl.loop(0, kv_heads)
        def _(h):
            hop(d, h).wait_send()

    @pl.loop(0, kv_heads)
    def _(h):
        give(h).wait()


def solution(mesh):
    sizes = (mesh.shape["outer"], mesh.shape["inner"])

    def shards(queries, keys, values, lengths, pack_order):
        rows = queries.shape[0]
        kv_heads = keys.shape[1] // HD
        group = queries.shape[1] // keys.shape[1]
        ndoc = lengths.shape[0]
        hbm = pl.BlockSpec(memory_space=pltpu.HBM)
        return pl.pallas_call(
            functools.partial(kernel, sizes),
            out_shape=jax.ShapeDtypeStruct(queries.shape, jnp.bfloat16),
            in_specs=[hbm] * 5,
            out_specs=hbm,
            scratch_shapes=[
                pltpu.VMEM((1, ndoc), jnp.int32),
                pltpu.VMEM((1, ndoc), jnp.int32),
                pltpu.VMEM(queries.shape, jnp.bfloat16),
                pltpu.VMEM(queries.shape, jnp.bfloat16),
                pltpu.VMEM((HOPS + 1, kv_heads, 2, rows, HD), jnp.bfloat16),
                pltpu.VMEM((kv_heads, group * rows, HD), jnp.float32),
                pltpu.VMEM((kv_heads, group * rows, 1), jnp.float32),
                pltpu.VMEM((kv_heads, group * rows, 1), jnp.float32),
                pltpu.VMEM((rows, HD), jnp.float32),
                pltpu.SemaphoreType.DMA((2,)),
                pltpu.SemaphoreType.DMA,
                pltpu.SemaphoreType.DMA((kv_heads, 2)),
                pltpu.SemaphoreType.DMA((kv_heads,)),
                pltpu.SemaphoreType.DMA((HOPS, kv_heads)),
                pltpu.SemaphoreType.DMA((HOPS, kv_heads)),
            ],
            compiler_params=pltpu.CompilerParams(
                collective_id=0, has_side_effects=True, vmem_limit_bytes=67043328),
            name="relay_attention",
        )(queries, keys, values, lengths.reshape(1, ndoc), pack_order.reshape(1, ndoc))

    return jax.shard_map(
        shards,
        mesh=mesh,
        in_specs=(P(("outer", "inner"), None),) * 3 + (P(), P()),
        out_specs=P(("outer", "inner"), None),
        check_vma=False,
    )
```

```python
import functools
import math

import jax
import jax.numpy as jnp
from jax import lax
from jax.experimental import pallas as pl
from jax.experimental.pallas import tpu as pltpu
from jax.sharding import PartitionSpec as P

HD = 128
HOPS = 8
RING = 32
LEG = (RING - HOPS) // 2
MESH = pl.DeviceIdType.MESH
SCALE = math.log2(math.e) / math.sqrt(HD)


def kernel(sizes, q_hbm, k_hbm, v_hbm, len_hbm, ord_hbm, o_hbm,
           len_ref, ord_ref, q_buf, o_buf, kv, mid_buf, acc, m_buf, l_buf, rel_buf, doc_sem, q_sem, in_sem, out_sem, send_sem, recv_sem,
           leg_send, leg_recv, back_send, back_recv, word):
    n_outer, n_inner = sizes
    rows = q_hbm.shape[0]
    kv_heads = k_hbm.shape[1] // HD
    group = q_hbm.shape[1] // k_hbm.shape[1]
    ndoc = len_hbm.shape[1]
    outer, inner = lax.axis_index("outer"), lax.axis_index("inner")
    device = outer * n_inner + inner
    total = n_outer * n_inner
    z = lax.rem(inner, RING)
    far = kv_heads - 1

    def place(index):
        index = lax.rem(index + total, total)
        return (index // n_inner, lax.rem(index, n_inner))

    right, left = place(device + 1), place(device - 1)
    first_middle = RING - HOPS - LEG
    is_source = z >= RING - HOPS
    is_middle = (z >= first_middle) & (z < first_middle + HOPS)
    is_start = z < HOPS

    def load(h, part):
        source = k_hbm if part == 0 else v_hbm
        columns = pl.ds(pl.multiple_of(h * HD, HD), HD)
        return pltpu.make_async_copy(source.at[:, columns], kv.at[0, h, part], in_sem.at[h, part])

    def give(h):
        columns = pl.ds(pl.multiple_of(h * group * HD, group * HD), group * HD)
        return pltpu.make_async_copy(o_buf.at[:, columns], o_hbm.at[:, columns], out_sem.at[h])

    def hop(d, h):
        return pltpu.make_async_remote_copy(
            src_ref=kv.at[d, h], dst_ref=kv.at[d + 1, h],
            send_sem=send_sem.at[d, h], recv_sem=recv_sem.at[d, h],
            device_id=right, device_id_type=MESH)

    def leg_one():
        return pltpu.make_async_remote_copy(
            src_ref=kv.at[0, far], dst_ref=mid_buf, send_sem=leg_send.at[0], recv_sem=leg_recv,
            device_id=place(device - LEG), device_id_type=MESH)

    def leg_two():
        return pltpu.make_async_remote_copy(
            src_ref=mid_buf, dst_ref=kv.at[HOPS, far], send_sem=leg_send.at[1], recv_sem=back_recv.at[HOPS],
            device_id=place(device + LEG + HOPS), device_id_type=MESH)

    def back(d):
        return pltpu.make_async_remote_copy(
            src_ref=kv.at[d, far], dst_ref=kv.at[d - 1, far], send_sem=back_send.at[d], recv_sem=back_recv.at[d - 1],
            device_id=left, device_id_type=MESH)

    def arrived(d):
        return pltpu.make_async_remote_copy(
            src_ref=kv.at[d, far], dst_ref=kv.at[d, far], send_sem=back_send.at[d], recv_sem=back_recv.at[d],
            device_id=left, device_id_type=MESH)

    @pl.loop(0, kv_heads)
    def _(h):
        load(h, 0).start()
        load(h, 1).start()

    len_copy = pltpu.make_async_copy(len_hbm, len_ref, doc_sem.at[0])
    ord_copy = pltpu.make_async_copy(ord_hbm, ord_ref, doc_sem.at[1])
    len_copy.start()
    ord_copy.start()
    q_copy = pltpu.make_async_copy(q_hbm, q_buf, q_sem)
    q_copy.start()

    barrier = pltpu.get_barrier_semaphore()

    def greet(neighbour):
        pl.semaphore_signal(barrier, inc=1, device_id=neighbour, device_id_type=MESH)

    greet(left)

    @pl.when(is_start)
    def _():
        greet(place(device - HOPS - LEG))

    @pl.when(z < HOPS - 1)
    def _():
        greet(right)

    two = is_middle | ((z > 0) & is_start)

    @pl.when(two)
    def _():
        pl.semaphore_wait(barrier, 2)

    @pl.when(jnp.logical_not(two))
    def _():
        pl.semaphore_wait(barrier, 1)

    load(far, 0).wait()
    load(far, 1).wait()

    @pl.loop(0, far)
    def _(h):
        load(h, 0).wait()
        load(h, 1).wait()
        hop(0, h).start()

    @pl.when(z < RING - 1)
    def _():
        hop(0, far).start()

    len_copy.wait()
    ord_copy.wait()
    sub = lax.broadcasted_iota(jnp.int32, (ndoc, ndoc), 0)
    lane = lax.broadcasted_iota(jnp.int32, (ndoc, ndoc), 1)
    lengths = jnp.broadcast_to(len_ref[...], (ndoc, ndoc))
    order = jnp.broadcast_to(ord_ref[...], (ndoc, ndoc))
    zero = jnp.zeros((ndoc, ndoc), jnp.float32)
    by_row = jnp.sum(jnp.where(sub == lane, lengths.astype(jnp.float32), zero), axis=1, keepdims=True)
    placed = jnp.sum(jnp.where(sub == order, jnp.broadcast_to(by_row, (ndoc, ndoc)), zero), axis=0, keepdims=True)
    placed = jnp.broadcast_to(placed, (ndoc, ndoc))
    placed = jnp.sum(jnp.where(sub == lane, placed, zero), axis=1, keepdims=True)
    placed = jnp.broadcast_to(placed, (ndoc, ndoc))
    starts = jnp.sum(jnp.where(sub < lane, placed, zero), axis=0, keepdims=True)
    first_row = (device * rows).astype(jnp.float32)
    starts = jnp.broadcast_to(starts - first_row, (rows, ndoc))
    token = lax.broadcasted_iota(jnp.int32, (rows, ndoc), 0).astype(jnp.float32)
    begin = jnp.max(jnp.where(starts <= token, starts, -first_row), axis=1, keepdims=True)
    rel_buf[...] = jnp.broadcast_to(begin, (rows, HD))

    q_copy.wait()
    key = lax.broadcasted_iota(jnp.int32, (rows, HD), 1).astype(jnp.float32)
    query = lax.broadcasted_iota(jnp.int32, (rows, HD), 0).astype(jnp.float32)

    def scores(d, h, mask):
        q = jnp.concatenate(
            [q_buf[:, pl.ds(pl.multiple_of((h * group + j) * HD, HD), HD)] for j in range(group)], axis=0)
        s = lax.dot_general(q, kv[d, h, 0], (((1,), (1,)), ((), ())), preferred_element_type=jnp.float32)
        s = jnp.where(mask[None], s.reshape(group, rows, HD), -jnp.inf)
        return s.reshape(group * rows, HD)

    def first(h, mask):
        s = scores(0, h, mask)
        m = jnp.max(s, axis=1, keepdims=True)
        p = jnp.exp2((s - m) * SCALE)
        m_buf[h] = m
        l_buf[h] = jnp.sum(p, axis=1, keepdims=True)
        acc[h] = jnp.dot(p.astype(jnp.bfloat16), kv[0, h, 1], preferred_element_type=jnp.float32)

    def later(d, h, mask):
        s = scores(d, h, mask)
        m_old = m_buf[h]
        m = jnp.maximum(m_old, jnp.max(s, axis=1, keepdims=True))
        p = jnp.exp2((s - m) * SCALE)
        alpha = jnp.exp2((m_old - m) * SCALE)
        total_p = alpha * l_buf[h] + jnp.sum(p, axis=1, keepdims=True)
        mixed = alpha * acc[h] + jnp.dot(p.astype(jnp.bfloat16), kv[d, h, 1], preferred_element_type=jnp.float32)
        return m, total_p, mixed

    own = (key >= rel_buf[...]) & (key <= query)

    @pl.loop(0, kv_heads)
    def _(h):
        first(h, own)

    def keep(d, h, mask):
        m, total_p, mixed = later(d, h, mask)
        m_buf[h] = m
        l_buf[h] = total_p
        acc[h] = mixed

    def finish(h, total_p, mixed):
        out = (mixed / total_p).astype(o_buf.dtype)
        for j in range(group):
            o_buf[:, pl.ds(pl.multiple_of((h * group + j) * HD, HD), HD)] = out[j * rows:(j + 1) * rows]
        give(h).start()

    def seen(d):
        return key - (d * rows).astype(jnp.float32) >= rel_buf[...]

    @pl.loop(1, HOPS)
    def _(d):
        mask = seen(d)

        @pl.loop(0, far)
        def _(h):
            tick = (d - 1) * far + h

            @pl.when((z >= first_middle) & (tick == (z - first_middle) // 2))
            def _():
                @pl.when(z > first_middle)
                def _():
                    pl.semaphore_wait(word, 1)

                @pl.when(z < RING - 1)
                def _():
                    pl.semaphore_signal(word, inc=1, device_id=right, device_id_type=MESH)

                @pl.when(is_source)
                def _():
                    leg_one().start()

            hop(d - 1, h).wait_recv()
            hop(d, h).start()
            keep(d, h, mask)

            @pl.when(is_middle & (tick == LEG + z - first_middle))
            def _():
                leg_one().wait_recv()
                leg_two().start()

            event = tick - 4 * far
            turn = (event - 1) // 2
            e = HOPS - turn

            @pl.when((event >= 1) & (event == turn * 2 + 1) & (e > z))
            def _():
                arrived(e).wait_recv()

                @pl.when(z > 0)
                def _():
                    back(e).start()

                keep(e, far, seen(e))

        @pl.when(z >= d)
        def _():
            hop(d - 1, far).wait_recv()

            @pl.when(z < RING - 1)
            def _():
                hop(d, far).start()

            keep(d, far, mask)

    last = seen(jnp.int32(HOPS))

    @pl.loop(0, far)
    def _(h):
        hop(HOPS - 1, h).wait_recv()
        m, total_p, mixed = later(HOPS, h, last)
        finish(h, total_p, mixed)

    @pl.when(z >= HOPS)
    def _():
        hop(HOPS - 1, far).wait_recv()
        keep(HOPS, far, last)

    finish(far, l_buf[far], acc[far])

    @pl.when(is_source)
    def _():
        leg_one().wait_send()

    @pl.when(is_middle)
    def _():
        leg_two().wait_send()

    @pl.loop(1, HOPS + 1)
    def _(d):
        @pl.when((z > 0) & (d > z))
        def _():
            back(d).wait_send()

    @pl.loop(0, HOPS)
    def _(d):
        @pl.when((z >= d) & (z < RING - 1))
        def _():
            hop(d, far).wait_send()

        @pl.loop(0, far)
        def _(h):
            hop(d, h).wait_send()

    @pl.loop(0, kv_heads)
    def _(h):
        give(h).wait()


def solution(mesh):
    sizes = (mesh.shape["outer"], mesh.shape["inner"])

    def shards(queries, keys, values, lengths, pack_order):
        rows = queries.shape[0]
        kv_heads = keys.shape[1] // HD
        group = queries.shape[1] // keys.shape[1]
        ndoc = lengths.shape[0]
        hbm = pl.BlockSpec(memory_space=pltpu.HBM)
        return pl.pallas_call(
            functools.partial(kernel, sizes),
            out_shape=jax.ShapeDtypeStruct(queries.shape, jnp.bfloat16),
            in_specs=[hbm] * 5,
            out_specs=hbm,
            scratch_shapes=[
                pltpu.VMEM((1, ndoc), jnp.int32),
                pltpu.VMEM((1, ndoc), jnp.int32),
                pltpu.VMEM(queries.shape, jnp.bfloat16),
                pltpu.VMEM(queries.shape, jnp.bfloat16),
                pltpu.VMEM((HOPS + 1, kv_heads, 2, rows, HD), jnp.bfloat16),
                pltpu.VMEM((2, rows, HD), jnp.bfloat16),
                pltpu.VMEM((kv_heads, group * rows, HD), jnp.float32),
                pltpu.VMEM((kv_heads, group * rows, 1), jnp.float32),
                pltpu.VMEM((kv_heads, group * rows, 1), jnp.float32),
                pltpu.VMEM((rows, HD), jnp.float32),
                pltpu.SemaphoreType.DMA((2,)),
                pltpu.SemaphoreType.DMA,
                pltpu.SemaphoreType.DMA((kv_heads, 2)),
                pltpu.SemaphoreType.DMA((kv_heads,)),
                pltpu.SemaphoreType.DMA((HOPS, kv_heads)),
                pltpu.SemaphoreType.DMA((HOPS, kv_heads)),
                pltpu.SemaphoreType.DMA((2,)),
                pltpu.SemaphoreType.DMA,
                pltpu.SemaphoreType.DMA((HOPS + 1,)),
                pltpu.SemaphoreType.DMA((HOPS + 1,)),
                pltpu.SemaphoreType.REGULAR,
            ],
            compiler_params=pltpu.CompilerParams(
                collective_id=0, has_side_effects=True, vmem_limit_bytes=67043328),
            name="relay_attention",
        )(queries, keys, values, lengths.reshape(1, ndoc), pack_order.reshape(1, ndoc))

    return jax.shard_map(
        shards,
        mesh=mesh,
        in_specs=(P(("outer", "inner"), None),) * 3 + (P(), P()),
        out_specs=P(("outer", "inner"), None),
        check_vma=False,
    )
```

```python
import functools
import math

import jax
import jax.numpy as jnp
from jax import lax
from jax.experimental import pallas as pl
from jax.experimental.pallas import tpu as pltpu
from jax.sharding import PartitionSpec as P

HD = 128
HOPS = 8
RING = 32
LEG = (RING - HOPS) // 2
MESH = pl.DeviceIdType.MESH
SCALE = math.log2(math.e) / math.sqrt(HD)


def kernel(sizes, q_hbm, k_hbm, v_hbm, len_hbm, ord_hbm, o_buf,
           len_ref, ord_ref, q_buf, kv, mid_buf, acc, m_buf, l_buf, rel_buf, doc_sem, q_sem, in_sem, send_sem, recv_sem,
           leg_send, leg_recv, back_send, back_recv, word):
    n_outer, n_inner = sizes
    rows = q_hbm.shape[0]
    kv_heads = k_hbm.shape[1] // HD
    group = q_hbm.shape[1] // k_hbm.shape[1]
    ndoc = len_hbm.shape[1]
    outer, inner = lax.axis_index("outer"), lax.axis_index("inner")
    device = outer * n_inner + inner
    total = n_outer * n_inner
    z = lax.rem(inner, RING)
    far = kv_heads - 1

    def place(index):
        index = lax.rem(index + total, total)
        return (index // n_inner, lax.rem(index, n_inner))

    right, left = place(device + 1), place(device - 1)
    first_middle = RING - HOPS - LEG
    is_source = z >= RING - HOPS
    is_middle = (z >= first_middle) & (z < first_middle + HOPS)
    is_start = z < HOPS

    def load(h, part):
        source = k_hbm if part == 0 else v_hbm
        columns = pl.ds(pl.multiple_of(h * HD, HD), HD)
        return pltpu.make_async_copy(source.at[:, columns], kv.at[0, h, part], in_sem.at[h, part])

    def hop(d, h):
        return pltpu.make_async_remote_copy(
            src_ref=kv.at[d, h], dst_ref=kv.at[d + 1, h],
            send_sem=send_sem.at[d, h], recv_sem=recv_sem.at[d, h],
            device_id=right, device_id_type=MESH)

    def leg_one():
        return pltpu.make_async_remote_copy(
            src_ref=kv.at[0, far], dst_ref=mid_buf, send_sem=leg_send.at[0], recv_sem=leg_recv,
            device_id=place(device - LEG), device_id_type=MESH)

    def leg_two():
        return pltpu.make_async_remote_copy(
            src_ref=mid_buf, dst_ref=kv.at[HOPS, far], send_sem=leg_send.at[1], recv_sem=back_recv.at[HOPS],
            device_id=place(device + LEG + HOPS), device_id_type=MESH)

    def back(d):
        return pltpu.make_async_remote_copy(
            src_ref=kv.at[d, far], dst_ref=kv.at[d - 1, far], send_sem=back_send.at[d], recv_sem=back_recv.at[d - 1],
            device_id=left, device_id_type=MESH)

    def arrived(d):
        return pltpu.make_async_remote_copy(
            src_ref=kv.at[d, far], dst_ref=kv.at[d, far], send_sem=back_send.at[d], recv_sem=back_recv.at[d],
            device_id=left, device_id_type=MESH)

    @pl.loop(0, kv_heads)
    def _(h):
        load(h, 0).start()
        load(h, 1).start()

    len_copy = pltpu.make_async_copy(len_hbm, len_ref, doc_sem.at[0])
    ord_copy = pltpu.make_async_copy(ord_hbm, ord_ref, doc_sem.at[1])
    len_copy.start()
    ord_copy.start()
    q_copy = pltpu.make_async_copy(q_hbm, q_buf, q_sem)
    q_copy.start()

    barrier = pltpu.get_barrier_semaphore()

    def greet(neighbour):
        pl.semaphore_signal(barrier, inc=1, device_id=neighbour, device_id_type=MESH)

    greet(left)

    @pl.when(is_start)
    def _():
        greet(place(device - HOPS - LEG))

    @pl.when(z < HOPS - 1)
    def _():
        greet(right)

    two = is_middle | ((z > 0) & is_start)

    @pl.when(two)
    def _():
        pl.semaphore_wait(barrier, 2)

    @pl.when(jnp.logical_not(two))
    def _():
        pl.semaphore_wait(barrier, 1)

    load(far, 0).wait()
    load(far, 1).wait()

    @pl.loop(0, far)
    def _(h):
        load(h, 0).wait()
        load(h, 1).wait()
        hop(0, h).start()

    @pl.when(z < RING - 1)
    def _():
        hop(0, far).start()

    len_copy.wait()
    ord_copy.wait()
    sub = lax.broadcasted_iota(jnp.int32, (ndoc, ndoc), 0)
    lane = lax.broadcasted_iota(jnp.int32, (ndoc, ndoc), 1)
    lengths = jnp.broadcast_to(len_ref[...], (ndoc, ndoc))
    order = jnp.broadcast_to(ord_ref[...], (ndoc, ndoc))
    zero = jnp.zeros((ndoc, ndoc), jnp.float32)
    by_row = jnp.sum(jnp.where(sub == lane, lengths.astype(jnp.float32), zero), axis=1, keepdims=True)
    placed = jnp.sum(jnp.where(sub == order, jnp.broadcast_to(by_row, (ndoc, ndoc)), zero), axis=0, keepdims=True)
    placed = jnp.broadcast_to(placed, (ndoc, ndoc))
    placed = jnp.sum(jnp.where(sub == lane, placed, zero), axis=1, keepdims=True)
    placed = jnp.broadcast_to(placed, (ndoc, ndoc))
    starts = jnp.sum(jnp.where(sub < lane, placed, zero), axis=0, keepdims=True)
    first_row = (device * rows).astype(jnp.float32)
    starts = jnp.broadcast_to(starts - first_row, (rows, ndoc))
    token = lax.broadcasted_iota(jnp.int32, (rows, ndoc), 0).astype(jnp.float32)
    begin = jnp.max(jnp.where(starts <= token, starts, -first_row), axis=1, keepdims=True)
    rel_buf[...] = jnp.broadcast_to(begin, (rows, HD))

    q_copy.wait()
    key = lax.broadcasted_iota(jnp.int32, (rows, HD), 1).astype(jnp.float32)
    query = lax.broadcasted_iota(jnp.int32, (rows, HD), 0).astype(jnp.float32)

    def scores(d, h, mask):
        q = jnp.concatenate(
            [q_buf[:, pl.ds(pl.multiple_of((h * group + j) * HD, HD), HD)] for j in range(group)], axis=0)
        s = lax.dot_general(q, kv[d, h, 0], (((1,), (1,)), ((), ())), preferred_element_type=jnp.float32)
        s = jnp.where(mask[None], s.reshape(group, rows, HD), -jnp.inf)
        return s.reshape(group * rows, HD)

    def first(h, mask):
        s = scores(0, h, mask)
        m = jnp.max(s, axis=1, keepdims=True)
        p = jnp.exp2((s - m) * SCALE)
        m_buf[h] = m
        l_buf[h] = jnp.sum(p, axis=1, keepdims=True)
        acc[h] = jnp.dot(p.astype(jnp.bfloat16), kv[0, h, 1], preferred_element_type=jnp.float32)

    def later(d, h, mask):
        s = scores(d, h, mask)
        m_old = m_buf[h]
        m = jnp.maximum(m_old, jnp.max(s, axis=1, keepdims=True))
        p = jnp.exp2((s - m) * SCALE)
        alpha = jnp.exp2((m_old - m) * SCALE)
        total_p = alpha * l_buf[h] + jnp.sum(p, axis=1, keepdims=True)
        mixed = alpha * acc[h] + jnp.dot(p.astype(jnp.bfloat16), kv[d, h, 1], preferred_element_type=jnp.float32)
        return m, total_p, mixed

    own = (key >= rel_buf[...]) & (key <= query)

    @pl.loop(0, kv_heads)
    def _(h):
        first(h, own)

    def keep(d, h, mask):
        m, total_p, mixed = later(d, h, mask)
        m_buf[h] = m
        l_buf[h] = total_p
        acc[h] = mixed

    def finish(h, total_p, mixed):
        out = (mixed / total_p).astype(o_buf.dtype)
        for j in range(group):
            o_buf[:, pl.ds(pl.multiple_of((h * group + j) * HD, HD), HD)] = out[j * rows:(j + 1) * rows]

    def seen(d):
        return key - (d * rows).astype(jnp.float32) >= rel_buf[...]

    @pl.loop(1, HOPS)
    def _(d):
        mask = seen(d)

        @pl.loop(0, far)
        def _(h):
            tick = (d - 1) * far + h

            @pl.when((z >= first_middle) & (tick == (z - first_middle) // 2))
            def _():
                @pl.when(z > first_middle)
                def _():
                    pl.semaphore_wait(word, 1)

                @pl.when(z < RING - 1)
                def _():
                    pl.semaphore_signal(word, inc=1, device_id=right, device_id_type=MESH)

                @pl.when(is_source)
                def _():
                    leg_one().start()

            hop(d - 1, h).wait_recv()
            hop(d, h).start()
            keep(d, h, mask)

            @pl.when(is_middle & (tick == LEG + z - first_middle))
            def _():
                leg_one().wait_recv()
                leg_two().start()

            event = tick - 4 * far
            turn = (event - 1) // 2
            e = HOPS - turn

            @pl.when((event >= 1) & (event == turn * 2 + 1) & (e > z))
            def _():
                arrived(e).wait_recv()

                @pl.when(z > 0)
                def _():
                    back(e).start()

                keep(e, far, seen(e))

        @pl.when(z >= d)
        def _():
            hop(d - 1, far).wait_recv()

            @pl.when(z < RING - 1)
            def _():
                hop(d, far).start()

            keep(d, far, mask)

    last = seen(jnp.int32(HOPS))

    @pl.loop(0, far)
    def _(h):
        hop(HOPS - 1, h).wait_recv()
        m, total_p, mixed = later(HOPS, h, last)
        finish(h, total_p, mixed)

    @pl.when(z >= HOPS)
    def _():
        hop(HOPS - 1, far).wait_recv()
        keep(HOPS, far, last)

    finish(far, l_buf[far], acc[far])

    @pl.when(is_source)
    def _():
        leg_one().wait_send()

    @pl.when(is_middle)
    def _():
        leg_two().wait_send()

    @pl.loop(1, HOPS + 1)
    def _(d):
        @pl.when((z > 0) & (d > z))
        def _():
            back(d).wait_send()

    @pl.loop(0, HOPS)
    def _(d):
        @pl.when((z >= d) & (z < RING - 1))
        def _():
            hop(d, far).wait_send()

        @pl.loop(0, far)
        def _(h):
            hop(d, h).wait_send()


def solution(mesh):
    sizes = (mesh.shape["outer"], mesh.shape["inner"])

    def shards(queries, keys, values, lengths, pack_order):
        rows = queries.shape[0]
        kv_heads = keys.shape[1] // HD
        group = queries.shape[1] // keys.shape[1]
        ndoc = lengths.shape[0]
        hbm = pl.BlockSpec(memory_space=pltpu.HBM)
        return pl.pallas_call(
            functools.partial(kernel, sizes),
            out_shape=jax.ShapeDtypeStruct(queries.shape, jnp.bfloat16),
            in_specs=[hbm] * 5,
            out_specs=pl.BlockSpec(memory_space=pltpu.VMEM),
            scratch_shapes=[
                pltpu.VMEM((1, ndoc), jnp.int32),
                pltpu.VMEM((1, ndoc), jnp.int32),
                pltpu.VMEM(queries.shape, jnp.bfloat16),
                pltpu.VMEM((HOPS + 1, kv_heads, 2, rows, HD), jnp.bfloat16),
                pltpu.VMEM((2, rows, HD), jnp.bfloat16),
                pltpu.VMEM((kv_heads, group * rows, HD), jnp.float32),
                pltpu.VMEM((kv_heads, group * rows, 1), jnp.float32),
                pltpu.VMEM((kv_heads, group * rows, 1), jnp.float32),
                pltpu.VMEM((rows, HD), jnp.float32),
                pltpu.SemaphoreType.DMA((2,)),
                pltpu.SemaphoreType.DMA,
                pltpu.SemaphoreType.DMA((kv_heads, 2)),
                pltpu.SemaphoreType.DMA((HOPS, kv_heads)),
                pltpu.SemaphoreType.DMA((HOPS, kv_heads)),
                pltpu.SemaphoreType.DMA((2,)),
                pltpu.SemaphoreType.DMA,
                pltpu.SemaphoreType.DMA((HOPS + 1,)),
                pltpu.SemaphoreType.DMA((HOPS + 1,)),
                pltpu.SemaphoreType.REGULAR,
            ],
            compiler_params=pltpu.CompilerParams(
                collective_id=0, has_side_effects=True, vmem_limit_bytes=50000000),
            name="relay_attention",
        )(*[pltpu.with_memory_space_constraint(x, pltpu.HBM) for x in (queries, keys, values, lengths.reshape(1, ndoc), pack_order.reshape(1, ndoc))])

    return jax.shard_map(
        shards,
        mesh=mesh,
        in_specs=(P(("outer", "inner"), None),) * 3 + (P(), P()),
        out_specs=P(("outer", "inner"), None),
        check_vma=False,
    )
```

```python
import functools
import math

import jax
import jax.numpy as jnp
from jax import lax
from jax.experimental import pallas as pl
from jax.experimental.pallas import tpu as pltpu
from jax.sharding import PartitionSpec as P

HD = 128
HOPS = 8
RING = 32
LEG = (RING - HOPS) // 2
MESH = pl.DeviceIdType.MESH
SCALE = math.log2(math.e) / math.sqrt(HD)


def kernel(sizes, q_hbm, k_hbm, v_hbm, len_hbm, ord_hbm, o_buf,
           len_ref, ord_ref, q_buf, kv, mid_buf, acc, m_buf, l_buf, rel_buf, doc_sem, q_sem, in_sem, send_sem, recv_sem,
           leg_send, leg_recv, back_send, back_recv, word):
    n_outer, n_inner = sizes
    rows = q_hbm.shape[0]
    kv_heads = k_hbm.shape[1] // HD
    group = q_hbm.shape[1] // k_hbm.shape[1]
    ndoc = len_hbm.shape[1]
    outer, inner = lax.axis_index("outer"), lax.axis_index("inner")
    device = outer * n_inner + inner
    total = n_outer * n_inner
    z = lax.rem(inner, RING)
    far = kv_heads - 1

    def place(index):
        index = lax.rem(index + total, total)
        return (index // n_inner, lax.rem(index, n_inner))

    right, left = place(device + 1), place(device - 1)
    first_middle = RING - HOPS - LEG
    is_source = z >= RING - HOPS
    is_middle = (z >= first_middle) & (z < first_middle + HOPS)
    is_start = z < HOPS

    def load(h, part):
        source = k_hbm if part == 0 else v_hbm
        columns = pl.ds(pl.multiple_of(h * HD, HD), HD)
        return pltpu.make_async_copy(source.at[:, columns], kv.at[0, h, part], in_sem.at[h, part])

    def hop(d, h):
        return pltpu.make_async_remote_copy(
            src_ref=kv.at[d, h], dst_ref=kv.at[d + 1, h],
            send_sem=send_sem.at[d, h], recv_sem=recv_sem.at[d, h],
            device_id=right, device_id_type=MESH)

    def leg_one():
        return pltpu.make_async_remote_copy(
            src_ref=kv.at[0, far], dst_ref=mid_buf, send_sem=leg_send.at[0], recv_sem=leg_recv,
            device_id=place(device - LEG), device_id_type=MESH)

    def leg_two():
        return pltpu.make_async_remote_copy(
            src_ref=mid_buf, dst_ref=kv.at[HOPS, far], send_sem=leg_send.at[1], recv_sem=back_recv.at[HOPS],
            device_id=place(device + LEG + HOPS), device_id_type=MESH)

    def back(d):
        return pltpu.make_async_remote_copy(
            src_ref=kv.at[d, far], dst_ref=kv.at[d - 1, far], send_sem=back_send.at[d], recv_sem=back_recv.at[d - 1],
            device_id=left, device_id_type=MESH)

    def arrived(d):
        return pltpu.make_async_remote_copy(
            src_ref=kv.at[d, far], dst_ref=kv.at[d, far], send_sem=back_send.at[d], recv_sem=back_recv.at[d],
            device_id=left, device_id_type=MESH)

    @pl.loop(0, kv_heads)
    def _(h):
        load(h, 0).start()
        load(h, 1).start()

    len_copy = pltpu.make_async_copy(len_hbm, len_ref, doc_sem.at[0])
    ord_copy = pltpu.make_async_copy(ord_hbm, ord_ref, doc_sem.at[1])
    len_copy.start()
    ord_copy.start()
    q_copy = pltpu.make_async_copy(q_hbm, q_buf, q_sem)
    q_copy.start()

    barrier = pltpu.get_barrier_semaphore()

    def greet(neighbour):
        pl.semaphore_signal(barrier, inc=1, device_id=neighbour, device_id_type=MESH)

    greet(left)

    @pl.when(is_start)
    def _():
        greet(place(device - HOPS - LEG))

    @pl.when(z < HOPS - 1)
    def _():
        greet(right)

    two = is_middle | ((z > 0) & is_start)

    @pl.when(two)
    def _():
        pl.semaphore_wait(barrier, 2)

    @pl.when(jnp.logical_not(two))
    def _():
        pl.semaphore_wait(barrier, 1)

    load(far, 0).wait()
    load(far, 1).wait()

    @pl.loop(0, far)
    def _(h):
        load(h, 0).wait()
        load(h, 1).wait()
        hop(0, h).start()

    @pl.when(z < RING - 1)
    def _():
        hop(0, far).start()

    len_copy.wait()
    ord_copy.wait()
    sub = lax.broadcasted_iota(jnp.int32, (ndoc, ndoc), 0)
    lane = lax.broadcasted_iota(jnp.int32, (ndoc, ndoc), 1)
    lengths = jnp.broadcast_to(len_ref[...], (ndoc, ndoc))
    order = jnp.broadcast_to(ord_ref[...], (ndoc, ndoc))
    zero = jnp.zeros((ndoc, ndoc), jnp.float32)
    by_row = jnp.sum(jnp.where(sub == lane, lengths.astype(jnp.float32), zero), axis=1, keepdims=True)
    placed = jnp.sum(jnp.where(sub == order, jnp.broadcast_to(by_row, (ndoc, ndoc)), zero), axis=0, keepdims=True)
    placed = jnp.broadcast_to(placed, (ndoc, ndoc))
    placed = jnp.sum(jnp.where(sub == lane, placed, zero), axis=1, keepdims=True)
    placed = jnp.broadcast_to(placed, (ndoc, ndoc))
    starts = jnp.sum(jnp.where(sub < lane, placed, zero), axis=0, keepdims=True)
    first_row = (device * rows).astype(jnp.float32)
    starts = jnp.broadcast_to(starts - first_row, (rows, ndoc))
    token = lax.broadcasted_iota(jnp.int32, (rows, ndoc), 0).astype(jnp.float32)
    begin = jnp.max(jnp.where(starts <= token, starts, -first_row), axis=1, keepdims=True)
    rel_buf[...] = jnp.broadcast_to(begin, (rows, HD))

    q_copy.wait()
    key = lax.broadcasted_iota(jnp.int32, (rows, HD), 1).astype(jnp.float32)
    query = lax.broadcasted_iota(jnp.int32, (rows, HD), 0).astype(jnp.float32)

    def scores(d, h, mask):
        q = jnp.concatenate(
            [q_buf[:, pl.ds(pl.multiple_of((h * group + j) * HD, HD), HD)] for j in range(group)], axis=0)
        s = lax.dot_general(q, kv[d, h, 0], (((1,), (1,)), ((), ())), preferred_element_type=jnp.float32)
        s = jnp.where(mask[None], s.reshape(group, rows, HD), -jnp.inf)
        return s.reshape(group * rows, HD)

    def first(h, mask):
        s = scores(0, h, mask)
        m = jnp.max(s, axis=1, keepdims=True)
        p = jnp.exp2((s - m) * SCALE)
        m_buf[h] = m
        l_buf[h] = jnp.sum(p, axis=1, keepdims=True)
        acc[h] = jnp.dot(p.astype(jnp.bfloat16), kv[0, h, 1], preferred_element_type=jnp.float32)

    def later(d, h, mask):
        s = scores(d, h, mask)
        m_old = m_buf[h]
        m = jnp.maximum(m_old, jnp.max(s, axis=1, keepdims=True))
        p = jnp.exp2((s - m) * SCALE)
        alpha = jnp.exp2((m_old - m) * SCALE)
        total_p = alpha * l_buf[h] + jnp.sum(p, axis=1, keepdims=True)
        mixed = alpha * acc[h] + jnp.dot(p.astype(jnp.bfloat16), kv[d, h, 1], preferred_element_type=jnp.float32)
        return m, total_p, mixed

    own = (key >= rel_buf[...]) & (key <= query)

    @pl.loop(0, kv_heads)
    def _(h):
        first(h, own)

    def keep(d, h, mask):
        m, total_p, mixed = later(d, h, mask)
        m_buf[h] = m
        l_buf[h] = total_p
        acc[h] = mixed

    def finish(h, total_p, mixed):
        out = (mixed / total_p).astype(o_buf.dtype)
        for j in range(group):
            o_buf[:, pl.ds(pl.multiple_of((h * group + j) * HD, HD), HD)] = out[j * rows:(j + 1) * rows]

    def seen(d):
        return key - (d * rows).astype(jnp.float32) >= rel_buf[...]

    @pl.loop(1, HOPS)
    def _(d):
        mask = seen(d)

        @pl.loop(0, far)
        def _(h):
            tick = (d - 1) * far + h

            @pl.when((z >= first_middle) & (tick == (z - first_middle) // 2))
            def _():
                @pl.when(z > first_middle)
                def _():
                    pl.semaphore_wait(word, 1)

                @pl.when(z < RING - 1)
                def _():
                    pl.semaphore_signal(word, inc=1, device_id=right, device_id_type=MESH)

                @pl.when(is_source)
                def _():
                    leg_one().start()

            hop(d - 1, h).wait_recv()
            hop(d, h).start()
            keep(d, h, mask)

            @pl.when(is_middle & (tick == LEG + z - first_middle))
            def _():
                leg_one().wait_recv()
                leg_two().start()

            event = tick - 4 * far
            turn = event // 2
            e = HOPS - turn

            @pl.when((event >= 0) & (event == turn * 2) & (e > z))
            def _():
                arrived(e).wait_recv()

                @pl.when(z > 0)
                def _():
                    back(e).start()

                keep(e, far, seen(e))

        @pl.when(z >= d)
        def _():
            hop(d - 1, far).wait_recv()

            @pl.when(z < RING - 1)
            def _():
                hop(d, far).start()

            keep(d, far, mask)

    last = seen(jnp.int32(HOPS))

    @pl.loop(0, far)
    def _(h):
        hop(HOPS - 1, h).wait_recv()
        m, total_p, mixed = later(HOPS, h, last)
        finish(h, total_p, mixed)

    @pl.when(z >= HOPS)
    def _():
        hop(HOPS - 1, far).wait_recv()
        keep(HOPS, far, last)

    finish(far, l_buf[far], acc[far])

    @pl.when(is_source)
    def _():
        leg_one().wait_send()

    @pl.when(is_middle)
    def _():
        leg_two().wait_send()

    @pl.loop(1, HOPS + 1)
    def _(d):
        @pl.when((z > 0) & (d > z))
        def _():
            back(d).wait_send()

    @pl.loop(0, HOPS)
    def _(d):
        @pl.when((z >= d) & (z < RING - 1))
        def _():
            hop(d, far).wait_send()

        @pl.loop(0, far)
        def _(h):
            hop(d, h).wait_send()


def solution(mesh):
    sizes = (mesh.shape["outer"], mesh.shape["inner"])

    def shards(queries, keys, values, lengths, pack_order):
        rows = queries.shape[0]
        kv_heads = keys.shape[1] // HD
        group = queries.shape[1] // keys.shape[1]
        ndoc = lengths.shape[0]
        hbm = pl.BlockSpec(memory_space=pltpu.HBM)
        return pl.pallas_call(
            functools.partial(kernel, sizes),
            out_shape=jax.ShapeDtypeStruct(queries.shape, jnp.bfloat16),
            in_specs=[hbm] * 5,
            out_specs=pl.BlockSpec(memory_space=pltpu.VMEM),
            scratch_shapes=[
                pltpu.VMEM((1, ndoc), jnp.int32),
                pltpu.VMEM((1, ndoc), jnp.int32),
                pltpu.VMEM(queries.shape, jnp.bfloat16),
                pltpu.VMEM((HOPS + 1, kv_heads, 2, rows, HD), jnp.bfloat16),
                pltpu.VMEM((2, rows, HD), jnp.bfloat16),
                pltpu.VMEM((kv_heads, group * rows, HD), jnp.float32),
                pltpu.VMEM((kv_heads, group * rows, 1), jnp.float32),
                pltpu.VMEM((kv_heads, group * rows, 1), jnp.float32),
                pltpu.VMEM((rows, HD), jnp.float32),
                pltpu.SemaphoreType.DMA((2,)),
                pltpu.SemaphoreType.DMA,
                pltpu.SemaphoreType.DMA((kv_heads, 2)),
                pltpu.SemaphoreType.DMA((HOPS, kv_heads)),
                pltpu.SemaphoreType.DMA((HOPS, kv_heads)),
                pltpu.SemaphoreType.DMA((2,)),
                pltpu.SemaphoreType.DMA,
                pltpu.SemaphoreType.DMA((HOPS + 1,)),
                pltpu.SemaphoreType.DMA((HOPS + 1,)),
                pltpu.SemaphoreType.REGULAR,
            ],
            compiler_params=pltpu.CompilerParams(
                collective_id=0, has_side_effects=True, vmem_limit_bytes=50000000),
            name="relay_attention",
        )(*[pltpu.with_memory_space_constraint(x, pltpu.HBM) for x in (queries, keys, values, lengths.reshape(1, ndoc), pack_order.reshape(1, ndoc))])

    return jax.shard_map(
        shards,
        mesh=mesh,
        in_specs=(P(("outer", "inner"), None),) * 3 + (P(), P()),
        out_specs=P(("outer", "inner"), None),
        check_vma=False,
    )
```
